32 devices in a mesh: clip: 2 (over y), tile: 4 (over z), tm: 2 (over x), chan: 2 (over core).
Axes of the slice: x: 2, y: 2, z: 4, core: 2. Of those that a mesh axis runs over, the one named last changes fastest.
Arguments:
- latent: bfloat16 [8, 8, 256, 128], P(('clip', 'tm'), 'tile', 'chan'), parts along dimension 0
- norm1_gain: float32 [256], P('chan'), may hold values from 0.25 to 1.75
- norm1_bias: float32 [256], P('chan'), may hold values from -3 to 3
- conv1_weight: bfloat16 [3, 3, 3, 256, 256], P(None, None, None, None, 'chan'), may hold values from -0.078125 to 0.078125
- conv1_bias: float32 [256], P('chan'), may hold values from -3 to 3
- norm2_gain: float32 [256], P('chan'), may hold values from 0.25 to 1.75
- norm2_bias: float32 [256], P('chan'), may hold values from -3 to 3
- conv2_weight: bfloat16 [3, 3, 3, 256, 256], P(None, None, None, None, 'chan'), may hold values from -0.078125 to 0.078125
- conv2_bias: float32 [256], P('chan'), may hold values from -3 to 3
Outputs:
- upsampled: bfloat16 [8, 16, 64, 256], P(('clip', 'tm'), 'tile', 'chan'), parts along dimension 0
The draws below stay inside these ranges and needn't reach their ends.
There are 2 independent parts, one for each index of `clip`. The reference program is written for one: setup_inputs(seed, part) draws one part's arguments, and reference() takes and returns one part's arrays. A program takes and returns all parts, laid end to end along the dimension named above; an argument that names none is the same for every part. Nothing has to cross between parts.
All inputs are finite; a program needn't handle non-finite values.
Results may differ from the reference program's by a relative error of at most 0.0026.
Values may be sent and summed in bfloat16 or wider, within the bound.
A program may use at most 64 MiB of HBM per device.

```python
import jax
import jax.numpy as jnp
from jax import lax

C = 256
GROUPS = 32
WIDE = 128
FRAMES = 4
HEIGHT = 8


def draw_latent(key, part):
    keys = jax.random.split(key, 3)
    shape = (FRAMES, HEIGHT, C, WIDE)
    rows = jnp.arange(HEIGHT, dtype=jnp.float32) / float(max(HEIGHT - 1, 1))
    rough = jax.random.uniform(keys[1], (HEIGHT,), jnp.float32, 0.6, 1.4)
    offset = jax.random.uniform(keys[2], (FRAMES, 1, C, 1), jnp.float32, -0.6, 0.6)
    base = jax.random.normal(keys[0], shape, jnp.float32)
    row_scale = jnp.exp(jnp.log(3.0) * rows) * rough
    values = base * row_scale[None, :, None, None] + offset
    return values.astype(jnp.bfloat16)


def block_scale(stream_key, dims, pieces, least, top_value):
    loudness = 1.0
    for axis_at, shards_of in pieces:
        steps = jax.random.uniform(jax.random.fold_in(jax.random.fold_in(stream_key, 6), axis_at), (shards_of,), jnp.float32, least / len(pieces), top_value / len(pieces))
        loudness = loudness * jnp.repeat(jnp.exp(steps), dims[axis_at] // shards_of).reshape((-1,) + (1,) * (len(dims) - 1 - axis_at))
    return loudness


def scatter_about(rng, extent, spread, most, cuts=(), held_as=jnp.bfloat16):
    values = spread * jax.random.normal(rng, extent, jnp.float32)
    if cuts:
        values = values * block_scale(rng, extent, cuts, -0.22, 0.18)
    return jnp.clip(values, -most, most).astype(held_as)


def setup_inputs(seed: int = 0, part: int = 0) -> dict:
    seeds = jax.random.split(jax.random.key(seed), 10)
    part_keys = jax.random.split(jax.random.fold_in(seeds[9], part), 10)
    return {
        "latent": draw_latent(jax.random.fold_in(jax.random.fold_in(seeds[9], part), 71), part),
        "norm1_gain": jnp.clip(1.0 + 0.15 * jax.random.normal(seeds[1], (C,), jnp.float32), 0.25, 1.75),
        "norm1_bias": scatter_about(seeds[2], (C,), 0.5, 3.0, ((0, 2),), jnp.float32),
        "conv1_weight": scatter_about(seeds[3], (3, 3, 3, C, C), (27 * C) ** -0.5, 0.078125, ((4, 2),)),
        "conv1_bias": scatter_about(seeds[4], (C,), 0.5, 3.0, ((0, 2),), jnp.float32),
        "norm2_gain": jnp.clip(1.0 + 0.15 * jax.random.normal(seeds[5], (C,), jnp.float32), 0.25, 1.75),
        "norm2_bias": scatter_about(seeds[6], (C,), 0.5, 3.0, ((0, 2),), jnp.float32),
        "conv2_weight": scatter_about(seeds[7], (3, 3, 3, C, C), (27 * C) ** -0.5, 0.078125, ((4, 2),)),
        "conv2_bias": scatter_about(seeds[8], (C,), 0.5, 3.0, ((0, 2),), jnp.float32),
    }


def causal_norm(field, gain, bias):
    frames, height, channels, columns = field.shape
    size = channels // GROUPS
    parts = field.reshape(frames, height, GROUPS, size, columns)
    totals = jnp.cumsum(lax.optimization_barrier(jnp.sum(parts, axis=(1, 3, 4))), axis=0)
    squares = jnp.cumsum(lax.optimization_barrier(jnp.sum(parts * parts, axis=(1, 3, 4))), axis=0)
    count = (jnp.arange(frames, dtype=jnp.float32) + 1.0) * float(height * size * columns)
    mean = totals / count[:, None]
    var = squares / count[:, None] - mean * mean
    scale = 1.0 / jnp.sqrt(var + 1e-06)
    normed = (parts - mean[:, None, :, None, None]) * scale[:, None, :, None, None]
    normed = normed.reshape(frames, height, channels, columns)
    return normed * gain[None, None, :, None] + bias[None, None, :, None]

def causal_conv(field, weight, bias):
    padded = jnp.concatenate([field[0:1], field[0:1], field], axis=0)
    source = jnp.transpose(padded, (2, 0, 1, 3))[None]
    result = lax.conv_general_dilated(source, weight, (1, 1, 1), ((0, 0), (1, 1), (1, 1)), dimension_numbers=('NCDHW', 'DHWIO', 'NCDHW'), preferred_element_type=jnp.float32)
    result = jnp.transpose(result[0], (1, 2, 0, 3))
    return result + bias[None, None, :, None]

def reference(latent, norm1_gain, norm1_bias, conv1_weight, conv1_bias, norm2_gain, norm2_bias, conv2_weight, conv2_bias):
    source = latent.astype(jnp.float32)
    first = jax.nn.silu(causal_norm(source, norm1_gain, norm1_bias)).astype(jnp.bfloat16)
    hidden = causal_conv(first, conv1_weight, conv1_bias)
    second = jax.nn.silu(causal_norm(hidden, norm2_gain, norm2_bias)).astype(jnp.bfloat16)
    mixed = source + causal_conv(second, conv2_weight, conv2_bias)
    frames, height, channels, columns = mixed.shape
    shaped = mixed.reshape(frames, height, channels // 4, 2, 2, columns)
    shaped = jnp.transpose(shaped, (0, 1, 3, 2, 5, 4))
    return shaped.reshape(frames, 2 * height, channels // 4, 2 * columns).astype(jnp.bfloat16)
```

```python
import functools

import jax
import jax.numpy as jnp
from jax import lax
from jax.experimental import pallas as pl
from jax.experimental.pallas import tpu as pltpu
from jax.sharding import PartitionSpec as P

MESH = pl.DeviceIdType.MESH
C = 256
GROUPS = 32
SIZE = C // GROUPS
F32 = jnp.float32
BF16 = jnp.bfloat16


def iota(shape, dim):
    return lax.broadcasted_iota(jnp.int32, shape, dim)


def column(row, n):
    wide = jnp.broadcast_to(row, (n, row.shape[-1]))
    return jnp.sum(jnp.where(iota(wide.shape, 0) == iota(wide.shape, 1), wide, 0.0), axis=1, keepdims=True)


def kernel(
    tiles,
    blocks,
    latent,
    n1g,
    n1b,
    w1,
    c1b,
    n2g,
    n2b,
    w2,
    c2b,
    out,
    w1v,
    w2v,
    w1t,
    w2t,
    lat,
    act1,
    hid,
    act2,
    mix,
    params,
    own_stats,
    stats,
    means,
    scales,
    w_sem,
    p_sem,
    x_send,
    z_send,
    d_send,
    a_recv,
    d_recv,
    hz_send,
    hd_send,
    h_recv,
    hd_recv,
    s_send,
    s_recv,
):
    cores = 2
    count_all = tiles * blocks * cores
    tm = lax.axis_index("tm")
    tile = lax.axis_index("tile")
    core = lax.axis_index("chan")
    other = 1 - core
    me = (tm * cores + core) * tiles + tile
    local = latent.shape[2]
    wide = latent.shape[3]
    groups = local // SIZE
    rows = latent.shape[1]

    def where_is(index):
        return {"tm": index // (cores * tiles), "chan": (index // tiles) % cores, "tile": index % tiles}

    load1 = pltpu.make_async_copy(w1, w1v, w_sem.at[0])
    load2 = pltpu.make_async_copy(w2, w2v, w_sem.at[1])
    load1.start()
    load2.start()

    barrier = pltpu.get_barrier_semaphore()

    def greet(step, carry):
        pl.semaphore_signal(
            barrier, inc=1, device_id=where_is(lax.rem(me + step, count_all)), device_id_type=MESH
        )
        return carry

    lax.fori_loop(1, count_all, greet, 0)
    for i, ref in enumerate((n1g, n1b, n2g, n2b, c1b)):
        params[core, i] = ref[...]
    lat[2, 1, core] = latent[:, 0]
    lat[2, 2, core] = latent[:, 1]
    pl.semaphore_wait(barrier, count_all - 1)

    def remote(src, dst, send, recv, **device):
        return pltpu.make_async_remote_copy(
            src_ref=src, dst_ref=dst, send_sem=send, recv_sem=recv, device_id=device, device_id_type=MESH
        )

    started = []

    def go(condition, copy):
        @pl.when(condition)
        def _():
            copy.start()

        started.append((condition, copy))

    always = core >= 0
    has_up = tile < tiles - 1
    has_down = tile > 0
    slots = [s for s in range(3) if blocks > 2 - s]
    before = [s for s in slots if s < 2]

    for s in reversed(before):
        for r in (0, 1):
            go(
                tm + (2 - s) < blocks,
                remote(latent.at[:, r], lat.at[s, 1 + r, core], x_send.at[s, r], a_recv.at[s, 1 + r],
                       tm=tm + (2 - s)),
            )
    go(has_up, remote(latent.at[:, 1], lat.at[2, 0, core], z_send.at[2, 0], a_recv.at[2, 0], tile=tile + 1))
    go(has_down, remote(latent.at[:, 0], lat.at[2, 3, core], z_send.at[2, 1], a_recv.at[2, 3], tile=tile - 1))
    for r in (0, 1):
        go(always, remote(latent.at[:, r], lat.at[2, 1 + r, core], d_send.at[2, 1 + r], d_recv.at[2, 1 + r],
                          chan=other))
    go(always, remote(params.at[core], params.at[core], p_sem.at[0], p_sem.at[1], chan=other))

    lanes = iota((groups, 128), 1)
    subs = iota((groups, 128), 0)

    def send_stats(which, field):
        row = jnp.zeros((1, 128), F32)
        for f in (0, 1):
            total = jnp.zeros((groups, wide), F32)
            square = jnp.zeros((groups, wide), F32)
            for r in (0, 1):
                v = field(f, r).reshape(groups, SIZE, wide)
                total = total + jnp.sum(v, axis=1)
                square = square + jnp.sum(v * v, axis=1)
            for kind, part in enumerate((total, square)):
                col = jnp.sum(part, axis=1, keepdims=True)
                at = kind * 2 * groups + f * groups
                row = row + jnp.sum(jnp.where(lanes == subs + at, col, 0.0), axis=0, keepdims=True)
        own_stats[which] = row
        stats[which, me] = row

        def send(step, carry):
            to = lax.rem(me + step, count_all)
            remote(own_stats.at[which], stats.at[which, me], s_send.at[which, to], s_recv.at[which, me],
                   **where_is(to)).start()
            return carry

        lax.fori_loop(1, count_all, send, 0)

    def wait_stats(which):
        def wait(step, carry):
            to = lax.rem(me + step, count_all)
            remote(own_stats.at[which], stats.at[which, to], s_send.at[which, to], s_recv.at[which, to],
                   **where_is(to)).wait()
            return carry

        lax.fori_loop(1, count_all, wait, 0)

    def make_norms(which, frames):
        ahead = frames // 2 - 1
        per_block = []
        for b in range(blocks):
            for c in range(cores):
                first = jnp.sum(stats[which, pl.ds((b * cores + c) * tiles, tiles)], axis=0)
                both = first + pltpu.roll(first, 128 - groups, 1)
                per_block.append((b, c, first, both))
        for e in range(frames):
            block = tm - ahead + e // 2
            later = jnp.logical_and(block >= 0, e % 2 == 1)
            block = jnp.maximum(block, 0)
            number = (block * 2 + later.astype(jnp.int32) + 1).astype(F32)
            count = number * float(rows * tiles * SIZE * wide)
            for c in range(cores):
                run = jnp.zeros((1, 128), F32)
                for b, cc, first, both in per_block:
                    if cc == c:
                        whole = jnp.logical_or(b < block, jnp.logical_and(b == block, later))
                        run = run + jnp.where(whole, both, jnp.where(b == block, first, 0.0))
                mean = run / count
                var = pltpu.roll(mean, 128 - 2 * groups, 1) - mean * mean
                scale = 1.0 / jnp.sqrt(var + 1e-06)
                diagonal = lanes == subs
                for ref, value in ((means, mean), (scales, scale)):
                    col = jnp.sum(jnp.where(diagonal, jnp.broadcast_to(value, lanes.shape), 0.0), axis=1,
                                  keepdims=True)
                    ref[e * cores + c] = jnp.broadcast_to(col, (groups, 128))

    def per_channel(ref, at):
        v = ref[at]
        return jnp.broadcast_to(v[:, None, :], (groups, SIZE, 128)).reshape(local, 128)

    def flip(src, dst):
        def one(j, carry):
            for i in range(3):
                for k in range(3):
                    dst[j, k * local:(k + 1) * local, i * C:(i + 1) * C] = src[i, j, k].T
            return carry

        lax.fori_loop(0, 3, one, 0)

    def silu(v):
        half = 0.5 * v
        return half + half * jnp.tanh(half)

    def conv(act, wt, o):
        acc = None
        for j in range(3):
            part = jnp.dot(
                wt[j], act[pl.ds(pl.multiple_of(o * C, C), 3 * C), j * wide:(j + 2) * wide],
                preferred_element_type=F32,
            )
            acc = part if acc is None else acc + part
        lane = iota((local, wide), 1)
        result = []
        for r in range(2):
            a = [acc[k * local:(k + 1) * local, r * wide:(r + 1) * wide] for k in range(3)]
            left = jnp.where(lane == 0, 0.0, pltpu.roll(a[0], 1, 1))
            right = jnp.where(lane == wide - 1, 0.0, pltpu.roll(a[2], wide - 1, 1))
            result.append(a[1] + left + right)
        return result

    send_stats(0, lambda f, r: latent[f, r].astype(F32))
    load1.wait()
    flip(w1v, w1t)

    def arrived(s, row, condition):
        got = remote(lat.at[s, row, core], lat.at[s, row, core], d_send.at[s, row], a_recv.at[s, row], chan=other)

        @pl.when(condition)
        def _():
            got.wait_recv()

        go(condition, remote(lat.at[s, row, core], lat.at[s, row, core], d_send.at[s, row], d_recv.at[s, row],
                             chan=other))

    arrivals = []
    for s in reversed(before):
        here = tm >= 2 - s
        for r in (0, 1):
            arrived(s, 1 + r, here)
            side, row, to = ((has_down, 3, tile - 1), (has_up, 0, tile + 1))[r]
            go(
                jnp.logical_and(here, side),
                remote(lat.at[s, 1 + r, core], lat.at[s, row, core], z_send.at[s, 1 - r], a_recv.at[s, row], tile=to),
            )
    for s in reversed(slots):
        here = tm >= 2 - s
        arrived(s, 0, jnp.logical_and(here, has_down))
        arrived(s, 3, jnp.logical_and(here, has_up))

    wait_stats(0)
    make_norms(0, 6)
    remote(params.at[core], params.at[other], p_sem.at[0], p_sem.at[1], chan=other).wait_recv()

    def row_here(row):
        return has_down if row == 0 else has_up if row == 3 else always

    for s in reversed(slots):
        for row in range(4):
            @pl.when(jnp.logical_and(tm >= 2 - s, row_here(row)))
            def _(s=s, row=row):
                remote(lat.at[s, row, core], lat.at[s, row, other], d_send.at[s, row], d_recv.at[s, row],
                       chan=other).wait_recv()

    def norm1(step, carry):
        e, c = step // cores, step % cores
        s, f = e // 2, e % 2
        f = jnp.where(tm - 2 + s < 0, 0, f)
        s = jnp.maximum(s, 2 - tm)
        mean = per_channel(means, step)
        gain = per_channel(scales, step) * column(params[c, 0], local)
        bias = column(params[c, 1], local)
        for row in range(4):
            v = lat[s, row, c, f].astype(F32)
            v = silu((v - mean) * gain + bias)
            v = jnp.where(row_here(row), v, 0.0)
            act1[pl.ds(pl.multiple_of(step * local, local), local), row * wide:(row + 1) * wide] = v.astype(BF16)
        return carry

    lax.fori_loop(0, 6 * cores, norm1, 0)

    def conv1(o, carry):
        for r, h in enumerate(conv(act1, w1t, o)):
            hid[1 + r, core, o] = h.astype(BF16)

            @pl.when(o >= 2)
            def _():
                mix[(o - 2) * 2 + r] = h
        return carry

    lax.fori_loop(0, 4, conv1, 0)

    go(has_up, remote(hid.at[2, core], hid.at[0, core], hz_send.at[0], h_recv.at[0], tile=tile + 1))
    go(has_down, remote(hid.at[1, core], hid.at[3, core], hz_send.at[1], h_recv.at[1], tile=tile - 1))
    for r in (1, 2):
        go(always, remote(hid.at[r, core], hid.at[r, core], hd_send.at[r], hd_recv.at[r], chan=other))
    bias1 = column(c1b[...], local)
    send_stats(1, lambda f, r: mix[f * 2 + r] + bias1)
    load2.wait()
    flip(w2v, w2t)
    for at, row, side in ((0, 0, has_down), (1, 3, has_up)):
        @pl.when(side)
        def _(at=at, row=row):
            remote(hid.at[row, core], hid.at[row, core], hd_send.at[row], h_recv.at[at], chan=other).wait_recv()

        go(side, remote(hid.at[row, core], hid.at[row, core], hd_send.at[row], hd_recv.at[row], chan=other))
    wait_stats(1)
    make_norms(1, 4)
    for row in (1, 2, 0, 3):
        @pl.when(row_here(row))
        def _(row=row):
            remote(hid.at[row, core], hid.at[row, other], hd_send.at[row], hd_recv.at[row], chan=other).wait_recv()

    def norm2(step, carry):
        e, c = step // cores, step % cores
        shift = column(params[c, 4], local) - per_channel(means, step)
        gain = per_channel(scales, step) * column(params[c, 2], local)
        bias = column(params[c, 3], local)
        for row in range(4):
            v = hid[row, c, e].astype(F32)
            v = silu((v + shift) * gain + bias)
            v = jnp.where(row_here(row), v, 0.0)
            act2[pl.ds(pl.multiple_of(step * local, local), local), row * wide:(row + 1) * wide] = v.astype(BF16)
        return carry

    lax.fori_loop(0, 4 * cores, norm2, 0)

    bias2 = column(c2b[...], local)

    def conv2(o, carry):
        for r, h in enumerate(conv(act2, w2t, o)):
            mix[o * 2 + r] = latent[o, r].astype(F32) + (h + bias2)
        return carry

    lax.fori_loop(0, 2, conv2, 0)

    a, b = iota((2 * wide, 2 * wide), 0), iota((2 * wide, 2 * wide), 1)
    spread = jnp.where(b == 2 * (a % wide) + a // wide, 1.0, 0.0).astype(BF16)
    for f in range(2):
        for r in range(2):
            for p in range(2):
                pair = [mix[f * 2 + r, pl.ds(2 * p + q, local // 4, stride=4), :].astype(BF16) for q in range(2)]
                out[f, 2 * r + p] = jnp.dot(
                    jnp.concatenate(pair, axis=1), spread, preferred_element_type=F32
                ).astype(BF16)

    for condition, copy in started:
        @pl.when(condition)
        def _(copy=copy):
            copy.wait_send()


def shards(tiles, blocks, latent, n1g, n1b, w1, c1b, n2g, n2b, w2, c2b):
    frames, rows, local, wide = latent.shape
    count = tiles * blocks * 2
    groups = local // SIZE
    vmem = pl.BlockSpec(memory_space=pltpu.VMEM)
    hbm = pl.BlockSpec(memory_space=pl.ANY)
    dma = pltpu.SemaphoreType.DMA
    row = lambda v: v.reshape(1, local)
    return pl.pallas_call(
        functools.partial(kernel, tiles, blocks),
        out_shape=jax.ShapeDtypeStruct((frames, 2 * rows, local // 4, 2 * wide), BF16),
        in_specs=[vmem, vmem, vmem, hbm, vmem, vmem, vmem, hbm, vmem],
        out_specs=vmem,
        scratch_shapes=[
            pltpu.VMEM(w1.shape, BF16),
            pltpu.VMEM(w2.shape, BF16),
            pltpu.VMEM((3, 3 * local, 3 * C), BF16),
            pltpu.VMEM((3, 3 * local, 3 * C), BF16),
            pltpu.VMEM((3, 4, 2, 2, local, wide), BF16),
            pltpu.VMEM((6 * C, 4 * wide), BF16),
            pltpu.VMEM((4, 2, 4, local, wide), BF16),
            pltpu.VMEM((4 * C, 4 * wide), BF16),
            pltpu.VMEM((4, local, wide), F32),
            pltpu.VMEM((2, 5, 1, local), F32),
            pltpu.VMEM((2, 1, 128), F32),
            pltpu.VMEM((2, count, 1, 128), F32),
            pltpu.VMEM((12, groups, 128), F32),
            pltpu.VMEM((12, groups, 128), F32),
            dma((2,)),
            dma((2,)),
            dma((2, 2)),
            dma((3, 2)),
            dma((3, 4)),
            dma((3, 4)),
            dma((3, 4)),
            dma((2,)),
            dma((4,)),
            dma((2,)),
            dma((4,)),
            dma((2, count)),
            dma((2, count)),
        ],
        compiler_params=pltpu.CompilerParams(
            collective_id=0, has_side_effects=True, vmem_limit_bytes=48 * 1024 * 1024
        ),
        name="block",
    )(latent, row(n1g), row(n1b), w1, row(c1b), row(n2g), row(n2b), w2, row(c2b))


def solution(mesh):
    return jax.shard_map(
        functools.partial(shards, mesh.shape["tile"], mesh.shape["tm"]),
        mesh=mesh,
        in_specs=(
            P(("clip", "tm"), "tile", "chan", None),
            P("chan"),
            P("chan"),
            P(None, None, None, None, "chan"),
            P("chan"),
            P("chan"),
            P("chan"),
            P(None, None, None, None, "chan"),
            P("chan"),
        ),
        out_specs=P(("clip", "tm"), "tile", "chan", None),
        check_vma=False,
    )
```

```python
import functools

import jax
import jax.numpy as jnp
from jax import lax
from jax.experimental import pallas as pl
from jax.experimental.pallas import tpu as pltpu
from jax.sharding import PartitionSpec as P

MESH = pl.DeviceIdType.MESH
C = 256
GROUPS = 32
SIZE = C // GROUPS
F32 = jnp.float32
BF16 = jnp.bfloat16


def iota(shape, dim):
    return lax.broadcasted_iota(jnp.int32, shape, dim)


def column(row, n):
    wide = jnp.broadcast_to(row, (n, row.shape[-1]))
    return jnp.sum(jnp.where(iota(wide.shape, 0) == iota(wide.shape, 1), wide, 0.0), axis=1, keepdims=True)


def kernel(
    tiles,
    blocks,
    latent,
    n1g,
    n1b,
    w1,
    c1b,
    n2g,
    n2b,
    w2,
    c2b,
    out,
    w1v,
    w2v,
    w1t,
    w2t,
    lat,
    act1,
    hid,
    act2,
    mix,
    params,
    own_stats,
    stats,
    means,
    scales,
    l_sem,
    w_sem,
    p_sem,
    x_send,
    z_send,
    d_send,
    a_recv,
    d_recv,
    hz_send,
    hd_send,
    h_recv,
    hd_recv,
    s_send,
    s_recv,
):
    cores = 2
    count_all = tiles * blocks * cores
    tm = lax.axis_index("tm")
    tile = lax.axis_index("tile")
    core = lax.axis_index("chan")
    other = 1 - core
    me = (tm * cores + core) * tiles + tile
    local = latent.shape[2]
    wide = latent.shape[3]
    groups = local // SIZE
    rows = latent.shape[1]

    def where_is(index):
        return {"tm": index // (cores * tiles), "chan": (index // tiles) % cores, "tile": index % tiles}

    def remote(src, dst, send, recv, **device):
        return pltpu.make_async_remote_copy(
            src_ref=src, dst_ref=dst, send_sem=send, recv_sem=recv, device_id=device, device_id_type=MESH
        )

    loads = [pltpu.make_async_copy(latent.at[:, r], lat.at[2, 1 + r, core], l_sem.at[r]) for r in (0, 1)]
    loads += [
        pltpu.make_async_copy(ref, params.at[core, i], l_sem.at[2 + i])
        for i, ref in enumerate((n1g, n1b, n2g, n2b, c1b, c2b))
    ]
    load1 = pltpu.make_async_copy(w1, w1v, w_sem.at[0])
    load2 = pltpu.make_async_copy(w2, w2v, w_sem.at[1])
    barrier = pltpu.get_barrier_semaphore()

    def greet(step, carry):
        pl.semaphore_signal(
            barrier, inc=1, device_id=where_is(lax.rem(me + step, count_all)), device_id_type=MESH
        )
        return carry

    lax.fori_loop(1, count_all, greet, 0)
    for copy in loads:
        copy.start()
    load1.start()
    load2.start()
    for copy in loads:
        copy.wait()

    started = []

    def go(condition, copy):
        @pl.when(condition)
        def _():
            copy.start()

        started.append((condition, copy))

    always = core >= 0
    has_up = tile < tiles - 1
    has_down = tile > 0
    slots = [s for s in range(3) if blocks > 2 - s]
    before = [s for s in slots if s < 2]

    def lat_copy(s, row, f, to_s, to_row, send, recv, **device):
        return remote(lat.at[s, row, core, f], lat.at[to_s, to_row, core, f], send, recv, **device)

    lanes = iota((groups, 128), 1)
    subs = iota((groups, 128), 0)

    def make_stats(which, field):
        row = jnp.zeros((1, 128), F32)
        for f in (0, 1):
            total = jnp.zeros((groups, wide), F32)
            square = jnp.zeros((groups, wide), F32)
            for r in (0, 1):
                v = field(f, r).reshape(groups, SIZE, wide)
                total = total + jnp.sum(v, axis=1)
                square = square + jnp.sum(v * v, axis=1)
            for kind, part in enumerate((total, square)):
                col = jnp.sum(part, axis=1, keepdims=True)
                at = kind * 2 * groups + f * groups
                row = row + jnp.sum(jnp.where(lanes == subs + at, col, 0.0), axis=0, keepdims=True)
        own_stats[which] = row
        stats[which, me] = row

    def send_stats(which):
        def send(step, carry):
            to = lax.rem(me + step, count_all)
            remote(own_stats.at[which], stats.at[which, me], s_send.at[which, to], s_recv.at[which, me],
                   **where_is(to)).start()
            return carry

        lax.fori_loop(1, count_all, send, 0)

    def wait_stats(which):
        def wait(step, carry):
            to = lax.rem(me + step, count_all)
            remote(own_stats.at[which], stats.at[which, to], s_send.at[which, to], s_recv.at[which, to],
                   **where_is(to)).wait()
            return carry

        lax.fori_loop(1, count_all, wait, 0)

    def make_norms(which, frames):
        ahead = frames // 2 - 1
        per_block = []
        for b in range(blocks):
            for c in range(cores):
                first = jnp.sum(stats[which, pl.ds((b * cores + c) * tiles, tiles)], axis=0)
                both = first + pltpu.roll(first, 128 - groups, 1)
                per_block.append((b, c, first, both))
        for e in range(frames):
            block = tm - ahead + e // 2
            later = jnp.logical_and(block >= 0, e % 2 == 1)
            block = jnp.maximum(block, 0)
            number = (block * 2 + later.astype(jnp.int32) + 1).astype(F32)
            count = number * float(rows * tiles * SIZE * wide)
            for c in range(cores):
                run = jnp.zeros((1, 128), F32)
                for b, cc, first, both in per_block:
                    if cc == c:
                        whole = jnp.logical_or(b < block, jnp.logical_and(b == block, later))
                        run = run + jnp.where(whole, both, jnp.where(b == block, first, 0.0))
                mean = run / count
                var = pltpu.roll(mean, 128 - 2 * groups, 1) - mean * mean
                scale = 1.0 / jnp.sqrt(var + 1e-06)
                diagonal = lanes == subs
                for ref, value in ((means, mean), (scales, scale)):
                    col = jnp.sum(jnp.where(diagonal, jnp.broadcast_to(value, lanes.shape), 0.0), axis=1,
                                  keepdims=True)
                    ref[e * cores + c] = jnp.broadcast_to(col, (groups, 128))

    def per_channel(ref, at):
        v = ref[at]
        return jnp.broadcast_to(v[:, None, :], (groups, SIZE, 128)).reshape(local, 128)

    def flip(src, dst):
        def one(j, carry):
            for i in range(3):
                for k in range(3):
                    dst[j, k * local:(k + 1) * local, i * C:(i + 1) * C] = src[i, j, k].T
            return carry

        lax.fori_loop(0, 3, one, 0)

    def silu(v):
        half = 0.5 * v
        return half + half * jnp.tanh(half)

    def conv(act, wt, o):
        acc = None
        for j in range(3):
            part = jnp.dot(
                wt[j], act[pl.ds(pl.multiple_of(o * C, C), 3 * C), j * wide:(j + 2) * wide],
                preferred_element_type=F32,
            )
            acc = part if acc is None else acc + part
        lane = iota((local, wide), 1)
        result = []
        for r in range(2):
            a = [acc[k * local:(k + 1) * local, r * wide:(r + 1) * wide] for k in range(3)]
            left = jnp.where(lane == 0, 0.0, pltpu.roll(a[0], 1, 1))
            right = jnp.where(lane == wide - 1, 0.0, pltpu.roll(a[2], wide - 1, 1))
            result.append(a[1] + left + right)
        return result

    make_stats(0, lambda f, r: lat[2, 1 + r, core, f].astype(F32))
    pl.semaphore_wait(barrier, count_all - 1)
    send_stats(0)

    for s in reversed(before):
        for f in (0, 1):
            for r in (0, 1):
                go(tm + (2 - s) < blocks,
                   lat_copy(2, 1 + r, f, s, 1 + r, x_send.at[s, r, f], a_recv.at[s, 1 + r, f], tm=tm + (2 - s)))
    for f in (0, 1):
        go(has_up, lat_copy(2, 2, f, 2, 0, z_send.at[2, 0, f], a_recv.at[2, 0, f], tile=tile + 1))
        go(has_down, lat_copy(2, 1, f, 2, 3, z_send.at[2, 1, f], a_recv.at[2, 3, f], tile=tile - 1))
    for f in (0, 1):
        for r in (1, 2):
            go(always, lat_copy(2, r, f, 2, r, d_send.at[2, r, f], d_recv.at[2, r, f], chan=other))
    go(always, remote(params.at[core], params.at[core], p_sem.at[0], p_sem.at[1], chan=other))

    load1.wait()
    flip(w1v, w1t)
    load2.wait()
    flip(w2v, w2t)

    def arrived(s, row, f, condition):
        copy = lat_copy(s, row, f, s, row, d_send.at[s, row, f], d_recv.at[s, row, f], chan=other)

        @pl.when(condition)
        def _():
            lat_copy(s, row, f, s, row, d_send.at[s, row, f], a_recv.at[s, row, f], chan=other).wait_recv()
            copy.start()

        started.append((condition, copy))

    def from_other(s, row, f, condition):
        @pl.when(condition)
        def _():
            remote(lat.at[s, row, core, f], lat.at[s, row, other, f], d_send.at[s, row, f], d_recv.at[s, row, f],
                   chan=other).wait_recv()

    def row_here(row):
        return has_down if row == 0 else has_up if row == 3 else always

    for f in (0, 1):
        for row in (0, 3):
            arrived(2, row, f, row_here(row))
    for s in reversed(before):
        here = tm >= 2 - s
        for f in (0, 1):
            for r in (0, 1):
                arrived(s, 1 + r, f, here)
                side, row, to = ((has_down, 3, tile - 1), (has_up, 0, tile + 1))[r]
                go(jnp.logical_and(here, side),
                   lat_copy(s, 1 + r, f, s, row, z_send.at[s, 1 - r, f], a_recv.at[s, row, f], tile=to))

    wait_stats(0)
    make_norms(0, 6)
    remote(params.at[core], params.at[other], p_sem.at[0], p_sem.at[1], chan=other).wait_recv()
    for f in (0, 1):
        for row in range(4):
            from_other(2, row, f, row_here(row))

    def norm1(first, rows_of):
        def one(step, carry):
            e, c = step // cores, step % cores
            s, f = e // 2, e % 2
            f = jnp.where(tm - 2 + s < 0, 0, f)
            s = jnp.maximum(s, 2 - tm)
            mean = per_channel(means, step)
            gain = per_channel(scales, step) * column(params[c, 0], local)
            bias = column(params[c, 1], local)
            for row in rows_of:
                v = lat[s, row, c, f].astype(F32)
                v = silu((v - mean) * gain + bias)
                if row in (0, 3):
                    v = jnp.where(row_here(row), v, 0.0)
                act1[pl.ds(pl.multiple_of(step * local, local), local), row * wide:(row + 1) * wide] = v.astype(BF16)
            return carry

        lax.fori_loop(first * cores, (first + 2) * cores, one, 0)

    norm1(4, range(4))
    for s in before:
        for f in (0, 1):
            for row in (0, 3):
                arrived(s, row, f, jnp.logical_and(tm >= 2 - s, row_here(row)))
    for s in before:
        for f in (0, 1):
            for row in (1, 2):
                from_other(s, row, f, tm >= 2 - s)
    norm1(2, (1, 2))
    for s in before:
        for f in (0, 1):
            for row in (0, 3):
                from_other(s, row, f, jnp.logical_and(tm >= 2 - s, row_here(row)))
    norm1(2, (0, 3))

    def repeat_first():
        first = act1[2 * C:3 * C]
        act1[0:C] = first
        act1[C:2 * C] = first

    if blocks > 2:
        @pl.when(tm >= 2)
        def _():
            norm1(0, range(4))

        pl.when(tm < 2)(repeat_first)
    else:
        repeat_first()

    def z_copy(o, up):
        at, row, to, landed = (0, 2, tile + 1, 0) if up else (1, 1, tile - 1, 3)
        return remote(hid.at[row, core, o], hid.at[landed, core, o], hz_send.at[at, o], h_recv.at[at, o], tile=to)

    def d_copy(o, row):
        return remote(hid.at[row, core, o], hid.at[row, core, o], hd_send.at[row, o], hd_recv.at[row, o], chan=other)

    def conv1(o, carry):
        for r, h in enumerate(conv(act1, w1t, o)):
            hid[1 + r, core, o] = h.astype(BF16)

            @pl.when(o >= 2)
            def _():
                mix[jnp.maximum(o - 2, 0) * 2 + r] = h

        pl.when(has_up)(lambda: z_copy(o, True).start())
        pl.when(has_down)(lambda: z_copy(o, False).start())
        d_copy(o, 1).start()
        d_copy(o, 2).start()
        return carry

    lax.fori_loop(2, 4, conv1, 0)
    bias1 = column(params[core, 4], local)
    make_stats(1, lambda f, r: mix[f * 2 + r] + bias1)
    send_stats(1)
    lax.fori_loop(0, 2, conv1, 0)

    for o in (2, 3, 0, 1):
        for at, row in ((0, 0), (1, 3)):
            @pl.when(row_here(row))
            def _(at=at, row=row, o=o):
                remote(hid.at[row, core, o], hid.at[row, core, o], hd_send.at[row, o], h_recv.at[at, o],
                       chan=other).wait_recv()
                d_copy(o, row).start()
    wait_stats(1)
    make_norms(1, 4)

    def got(o, row):
        remote(hid.at[row, core, o], hid.at[row, other, o], hd_send.at[row, o], hd_recv.at[row, o],
               chan=other).wait_recv()

    def norm2(step, carry):
        e, c = step // cores, step % cores
        shift = column(params[c, 4], local) - per_channel(means, step)
        gain = per_channel(scales, step) * column(params[c, 2], local)
        bias = column(params[c, 3], local)
        for row in range(4):
            v = hid[row, c, e].astype(F32)
            v = silu((v + shift) * gain + bias)
            if row in (0, 3):
                v = jnp.where(row_here(row), v, 0.0)
            act2[pl.ds(pl.multiple_of(step * local, local), local), row * wide:(row + 1) * wide] = v.astype(BF16)
        return carry

    for o in (2, 3, 0, 1):
        got(o, 1)
        got(o, 2)
        pl.when(has_down)(lambda o=o: got(o, 0))
        pl.when(has_up)(lambda o=o: got(o, 3))
    lax.fori_loop(0, 4 * cores, norm2, 0)

    bias2 = column(params[core, 5], local)

    def conv2(o, carry):
        for r, h in enumerate(conv(act2, w2t, o)):
            mix[o * 2 + r] = lat[2, 1 + r, core, o].astype(F32) + (h + bias2)
        return carry

    lax.fori_loop(0, 2, conv2, 0)

    a, b = iota((2 * wide, 2 * wide), 0), iota((2 * wide, 2 * wide), 1)
    spread = jnp.where(b == 2 * (a % wide) + a // wide, 1.0, 0.0).astype(BF16)
    for f in range(2):
        for r in range(2):
            for p in range(2):
                pair = [mix[f * 2 + r, pl.ds(2 * p + q, local // 4, stride=4), :].astype(BF16) for q in range(2)]
                out[f, 2 * r + p] = jnp.dot(
                    jnp.concatenate(pair, axis=1), spread, preferred_element_type=F32
                ).astype(BF16)

    for condition, copy in started:
        @pl.when(condition)
        def _(copy=copy):
            copy.wait_send()

    for o in range(4):
        pl.when(has_up)(lambda o=o: z_copy(o, True).wait_send())
        pl.when(has_down)(lambda o=o: z_copy(o, False).wait_send())
        for row in range(4):
            pl.when(row_here(row))(lambda o=o, row=row: d_copy(o, row).wait_send())


def shards(tiles, blocks, latent, n1g, n1b, w1, c1b, n2g, n2b, w2, c2b):
    frames, rows, local, wide = latent.shape
    count = tiles * blocks * 2
    groups = local // SIZE
    vmem = pl.BlockSpec(memory_space=pltpu.VMEM)
    hbm = pl.BlockSpec(memory_space=pl.ANY)
    dma = pltpu.SemaphoreType.DMA
    row = lambda v: v.reshape(1, local)
    return pl.pallas_call(
        functools.partial(kernel, tiles, blocks),
        out_shape=jax.ShapeDtypeStruct((frames, 2 * rows, local // 4, 2 * wide), BF16),
        in_specs=[hbm] * 9,
        out_specs=vmem,
        scratch_shapes=[
            pltpu.VMEM(w1.shape, BF16),
            pltpu.VMEM(w2.shape, BF16),
            pltpu.VMEM((3, 3 * local, 3 * C), BF16),
            pltpu.VMEM((3, 3 * local, 3 * C), BF16),
            pltpu.VMEM((3, 4, 2, 2, local, wide), BF16),
            pltpu.VMEM((6 * C, 4 * wide), BF16),
            pltpu.VMEM((4, 2, 4, local, wide), BF16),
            pltpu.VMEM((4 * C, 4 * wide), BF16),
            pltpu.VMEM((4, local, wide), F32),
            pltpu.VMEM((2, 6, 1, local), F32),
            pltpu.VMEM((2, 1, 128), F32),
            pltpu.VMEM((2, count, 1, 128), F32),
            pltpu.VMEM((12, groups, 128), F32),
            pltpu.VMEM((12, groups, 128), F32),
            dma((8,)),
            dma((2,)),
            dma((2,)),
            dma((2, 2, 2)),
            dma((3, 2, 2)),
            dma((3, 4, 2)),
            dma((3, 4, 2)),
            dma((3, 4, 2)),
            dma((2, 4)),
            dma((4, 4)),
            dma((2, 4)),
            dma((4, 4)),
            dma((2, count)),
            dma((2, count)),
        ],
        compiler_params=pltpu.CompilerParams(
            collective_id=0, has_side_effects=True, vmem_limit_bytes=67_000_000
        ),
        name="block",
    )(latent, row(n1g), row(n1b), w1, row(c1b), row(n2g), row(n2b), w2, row(c2b))


def solution(mesh):
    return jax.shard_map(
        functools.partial(shards, mesh.shape["tile"], mesh.shape["tm"]),
        mesh=mesh,
        in_specs=(
            P(("clip", "tm"), "tile", "chan", None),
            P("chan"),
            P("chan"),
            P(None, None, None, None, "chan"),
            P("chan"),
            P("chan"),
            P("chan"),
            P(None, None, None, None, "chan"),
            P("chan"),
        ),
        out_specs=P(("clip", "tm"), "tile", "chan", None),
        check_vma=False,
    )
```

```python
import functools

import jax
import jax.numpy as jnp
from jax import lax
from jax.experimental import pallas as pl
from jax.experimental.pallas import tpu as pltpu
from jax.sharding import PartitionSpec as P

MESH = pl.DeviceIdType.MESH
C = 256
GROUPS = 32
SIZE = C // GROUPS
F32 = jnp.float32
BF16 = jnp.bfloat16


def iota(shape, dim):
    return lax.broadcasted_iota(jnp.int32, shape, dim)


def column(row, n):
    wide = jnp.broadcast_to(row, (n, row.shape[-1]))
    return jnp.sum(jnp.where(iota(wide.shape, 0) == iota(wide.shape, 1), wide, 0.0), axis=1, keepdims=True)


def kernel(
    tiles,
    blocks,
    latent,
    n1g,
    n1b,
    w1,
    c1b,
    n2g,
    n2b,
    w2,
    c2b,
    out,
    w1v,
    w2v,
    w1t,
    w2t,
    lat,
    act1,
    hid,
    act2,
    mix,
    select,
    params,
    own_stats,
    stats,
    means,
    scales,
    l_sem,
    w_sem,
    p_sem,
    x_send,
    z_send,
    d_send,
    a_recv,
    d_recv,
    hz_send,
    hd_send,
    h_recv,
    hd_recv,
    s_send,
    s_recv,
):
    cores = 2
    count_all = tiles * blocks * cores
    tm = lax.axis_index("tm")
    tile = lax.axis_index("tile")
    core = lax.axis_index("chan")
    other = 1 - core
    me = (tm * cores + core) * tiles + tile
    local = latent.shape[2]
    wide = latent.shape[3]
    groups = local // SIZE
    rows = latent.shape[1]

    def where_is(index):
        return {"tm": index // (cores * tiles), "chan": (index // tiles) % cores, "tile": index % tiles}

    def remote(src, dst, send, recv, **device):
        return pltpu.make_async_remote_copy(
            src_ref=src, dst_ref=dst, send_sem=send, recv_sem=recv, device_id=device, device_id_type=MESH
        )

    loads = [pltpu.make_async_copy(latent.at[:, r], lat.at[2, 1 + r, core], l_sem.at[r]) for r in (0, 1)]
    loads += [
        pltpu.make_async_copy(ref, params.at[core, i], l_sem.at[2 + i])
        for i, ref in enumerate((n1g, n1b, n2g, n2b, c1b, c2b))
    ]
    load1 = pltpu.make_async_copy(w1, w1v, w_sem.at[0])
    load2 = pltpu.make_async_copy(w2, w2v, w_sem.at[1])
    barrier = pltpu.get_barrier_semaphore()

    def greet(step, carry):
        pl.semaphore_signal(
            barrier, inc=1, device_id=where_is(lax.rem(me + step, count_all)), device_id_type=MESH
        )
        return carry

    lax.fori_loop(1, count_all, greet, 0)
    for copy in loads:
        copy.start()
    load1.start()
    load2.start()
    for copy in loads:
        copy.wait()

    started = []

    def go(condition, copy):
        @pl.when(condition)
        def _():
            copy.start()

        started.append((condition, copy))

    always = core >= 0
    has_up = tile < tiles - 1
    has_down = tile > 0
    slots = [s for s in range(3) if blocks > 2 - s]
    before = [s for s in slots if s < 2]

    def lat_copy(s, row, f, to_s, to_row, send, recv, **device):
        return remote(lat.at[s, row, core, f], lat.at[to_s, to_row, core, f], send, recv, **device)

    lanes = iota((groups, 128), 1)
    subs = iota((groups, 128), 0)

    def make_stats(which, field):
        row = jnp.zeros((1, 128), F32)
        for f in (0, 1):
            total = jnp.zeros((groups, wide), F32)
            square = jnp.zeros((groups, wide), F32)
            for r in (0, 1):
                v = field(f, r).reshape(groups, SIZE, wide)
                total = total + jnp.sum(v, axis=1)
                square = square + jnp.sum(v * v, axis=1)
            for kind, part in enumerate((total, square)):
                col = jnp.sum(part, axis=1, keepdims=True)
                at = kind * 2 * groups + f * groups
                row = row + jnp.sum(jnp.where(lanes == subs + at, col, 0.0), axis=0, keepdims=True)
        own_stats[which] = row
        stats[which, me] = row

    def send_stats(which):
        def send(step, carry):
            to = lax.rem(me + step, count_all)
            remote(own_stats.at[which], stats.at[which, me], s_send.at[which, to], s_recv.at[which, me],
                   **where_is(to)).start()
            return carry

        lax.fori_loop(1, count_all, send, 0)

    def wait_stats(which):
        def wait(step, carry):
            to = lax.rem(me + step, count_all)
            remote(own_stats.at[which], stats.at[which, to], s_send.at[which, to], s_recv.at[which, to],
                   **where_is(to)).wait()
            return carry

        lax.fori_loop(1, count_all, wait, 0)

    def make_norms(which, frames):
        ahead = frames // 2 - 1
        per_block = []
        for b in range(blocks):
            for c in range(cores):
                first = jnp.sum(stats[which, pl.ds((b * cores + c) * tiles, tiles)], axis=0)
                both = first + pltpu.roll(first, 128 - groups, 1)
                per_block.append((b, c, first, both))
        for e in range(frames):
            block = tm - ahead + e // 2
            later = jnp.logical_and(block >= 0, e % 2 == 1)
            block = jnp.maximum(block, 0)
            number = (block * 2 + later.astype(jnp.int32) + 1).astype(F32)
            count = number * float(rows * tiles * SIZE * wide)
            for c in range(cores):
                run = jnp.zeros((1, 128), F32)
                for b, cc, first, both in per_block:
                    if cc == c:
                        whole = jnp.logical_or(b < block, jnp.logical_and(b == block, later))
                        run = run + jnp.where(whole, both, jnp.where(b == block, first, 0.0))
                mean = run / count
                var = pltpu.roll(mean, 128 - 2 * groups, 1) - mean * mean
                scale = 1.0 / jnp.sqrt(var + 1e-06)
                diagonal = lanes == subs
                for ref, value in ((means, mean), (scales, scale)):
                    col = jnp.sum(jnp.where(diagonal, jnp.broadcast_to(value, lanes.shape), 0.0), axis=1,
                                  keepdims=True)
                    ref[e * cores + c] = jnp.broadcast_to(col, (groups, 128))

    def per_channel(ref, at):
        v = ref[at]
        return jnp.broadcast_to(v[:, None, :], (groups, SIZE, 128)).reshape(local, 128)

    def flip(src, dst):
        def one(j, carry):
            for i in range(3):
                for k in range(3):
                    dst[j, k * local:(k + 1) * local, i * C:(i + 1) * C] = src[i, j, k].T
            return carry

        lax.fori_loop(0, 3, one, 0)

    def silu_of_twice(half):
        return half + half * jnp.tanh(half)

    def clear_edges(act):
        for side, row in ((has_down, 0), (has_up, 3)):
            @pl.when(jnp.logical_not(side))
            def _(row=row):
                act[:, row * wide:(row + 1) * wide] = jnp.zeros((act.shape[0], wide), BF16)

    def conv(act, wt, o):
        acc = None
        for j in range(3):
            part = jnp.dot(
                wt[j], act[pl.ds(pl.multiple_of(o * C, C), 3 * C), j * wide:(j + 2) * wide],
                preferred_element_type=F32,
            )
            acc = part if acc is None else acc + part
        lane = iota((local, wide), 1)
        result = []
        for r in range(2):
            a = [acc[k * local:(k + 1) * local, r * wide:(r + 1) * wide] for k in range(3)]
            left = jnp.where(lane == 0, 0.0, pltpu.roll(a[0], 1, 1))
            right = jnp.where(lane == wide - 1, 0.0, pltpu.roll(a[2], wide - 1, 1))
            result.append(a[1] + left + right)
        return result

    make_stats(0, lambda f, r: lat[2, 1 + r, core, f].astype(F32))
    pl.semaphore_wait(barrier, count_all - 1)
    send_stats(0)

    for s in reversed(before):
        for f in (0, 1):
            for r in (0, 1):
                go(tm + (2 - s) < blocks,
                   lat_copy(2, 1 + r, f, s, 1 + r, x_send.at[s, r, f], a_recv.at[s, 1 + r, f], tm=tm + (2 - s)))
    for f in (0, 1):
        go(has_up, lat_copy(2, 2, f, 2, 0, z_send.at[2, 0, f], a_recv.at[2, 0, f], tile=tile + 1))
        go(has_down, lat_copy(2, 1, f, 2, 3, z_send.at[2, 1, f], a_recv.at[2, 3, f], tile=tile - 1))
    for f in (0, 1):
        for r in (1, 2):
            go(always, lat_copy(2, r, f, 2, r, d_send.at[2, r, f], d_recv.at[2, r, f], chan=other))
    go(always, remote(params.at[core], params.at[core], p_sem.at[0], p_sem.at[1], chan=other))

    a, b = iota((2 * wide, 2 * wide), 0), iota((2 * wide, 2 * wide), 1)
    select[...] = jnp.where(b == 2 * (a % wide) + a // wide, 1.0, 0.0).astype(BF16)
    load1.wait()
    flip(w1v, w1t)
    load2.wait()
    flip(w2v, w2t)

    def arrived(s, row, f, condition):
        copy = lat_copy(s, row, f, s, row, d_send.at[s, row, f], d_recv.at[s, row, f], chan=other)

        @pl.when(condition)
        def _():
            lat_copy(s, row, f, s, row, d_send.at[s, row, f], a_recv.at[s, row, f], chan=other).wait_recv()
            copy.start()

        started.append((condition, copy))

    def from_other(s, row, f, condition):
        @pl.when(condition)
        def _():
            remote(lat.at[s, row, core, f], lat.at[s, row, other, f], d_send.at[s, row, f], d_recv.at[s, row, f],
                   chan=other).wait_recv()

    def row_here(row):
        return has_down if row == 0 else has_up if row == 3 else always

    for s in reversed(before):
        here = tm >= 2 - s
        for f in (0, 1):
            for r in (0, 1):
                arrived(s, 1 + r, f, here)
                side, row, to = ((has_down, 3, tile - 1), (has_up, 0, tile + 1))[r]
                go(jnp.logical_and(here, side),
                   lat_copy(s, 1 + r, f, s, row, z_send.at[s, 1 - r, f], a_recv.at[s, row, f], tile=to))

    for f in (0, 1):
        for row in (0, 3):
            arrived(2, row, f, row_here(row))

    wait_stats(0)
    make_norms(0, 6)
    remote(params.at[core], params.at[other], p_sem.at[0], p_sem.at[1], chan=other).wait_recv()
    for f in (0, 1):
        for row in range(4):
            from_other(2, row, f, row_here(row))

    def norm1(first, rows_of):
        def one(step, carry):
            e, c = step // cores, step % cores
            s, f = e // 2, e % 2
            f = jnp.where(tm - 2 + s < 0, 0, f)
            s = jnp.maximum(s, 2 - tm)
            gain = per_channel(scales, step) * column(0.5 * params[c, 0], local)
            bias = column(0.5 * params[c, 1], local) - per_channel(means, step) * gain
            for row in rows_of:
                v = silu_of_twice(lat[s, row, c, f].astype(F32) * gain + bias)
                act1[pl.ds(pl.multiple_of(step * local, local), local), row * wide:(row + 1) * wide] = v.astype(BF16)
            return carry

        lax.fori_loop(first * cores, (first + 2) * cores, one, 0)

    norm1(4, range(4))
    for s in before:
        for f in (0, 1):
            for row in (0, 3):
                arrived(s, row, f, jnp.logical_and(tm >= 2 - s, row_here(row)))
    for s in before:
        for f in (0, 1):
            for row in (1, 2):
                from_other(s, row, f, tm >= 2 - s)
    norm1(2, (1, 2))
    for s in before:
        for f in (0, 1):
            for row in (0, 3):
                from_other(s, row, f, jnp.logical_and(tm >= 2 - s, row_here(row)))
    norm1(2, (0, 3))

    def repeat_first():
        first = act1[2 * C:3 * C]
        act1[0:C] = first
        act1[C:2 * C] = first

    if blocks > 2:
        @pl.when(tm >= 2)
        def _():
            norm1(0, range(4))

        pl.when(tm < 2)(repeat_first)
    else:
        repeat_first()

    clear_edges(act1)

    def z_copy(o, up):
        at, row, to, landed = (0, 2, tile + 1, 0) if up else (1, 1, tile - 1, 3)
        return remote(hid.at[row, core, o], hid.at[landed, core, o], hz_send.at[at, o], h_recv.at[at, o], tile=to)

    def d_copy(o, row):
        return remote(hid.at[row, core, o], hid.at[row, core, o], hd_send.at[row, o], hd_recv.at[row, o], chan=other)

    def conv1(o, carry):
        for r, h in enumerate(conv(act1, w1t, o)):
            hid[1 + r, core, o] = h.astype(BF16)

            @pl.when(o >= 2)
            def _():
                mix[jnp.maximum(o - 2, 0) * 2 + r] = h

        pl.when(has_up)(lambda: z_copy(o, True).start())
        pl.when(has_down)(lambda: z_copy(o, False).start())
        d_copy(o, 1).start()
        d_copy(o, 2).start()
        return carry

    lax.fori_loop(2, 4, conv1, 0)
    bias1 = column(params[core, 4], local)
    make_stats(1, lambda f, r: mix[f * 2 + r] + bias1)
    send_stats(1)
    lax.fori_loop(0, 2, conv1, 0)

    for o in (2, 3, 0, 1):
        for at, row in ((0, 0), (1, 3)):
            @pl.when(row_here(row))
            def _(at=at, row=row, o=o):
                remote(hid.at[row, core, o], hid.at[row, core, o], hd_send.at[row, o], h_recv.at[at, o],
                       chan=other).wait_recv()
                d_copy(o, row).start()
    wait_stats(1)
    make_norms(1, 4)

    def got(o, row):
        remote(hid.at[row, core, o], hid.at[row, other, o], hd_send.at[row, o], hd_recv.at[row, o],
               chan=other).wait_recv()

    def norm2(rows_of, step, carry):
        e, c = step // cores, step % cores
        gain = per_channel(scales, step) * column(0.5 * params[c, 2], local)
        bias = column(0.5 * params[c, 3], local) + (column(params[c, 4], local) - per_channel(means, step)) * gain
        for row in rows_of:
            v = silu_of_twice(hid[row, c, e].astype(F32) * gain + bias)
            act2[pl.ds(pl.multiple_of(step * local, local), local), row * wide:(row + 1) * wide] = v.astype(BF16)
        return carry

    for o in (2, 3, 0, 1):
        got(o, 1)
        got(o, 2)
    lax.fori_loop(0, 4 * cores, functools.partial(norm2, (1, 2)), 0)
    for o in (2, 3, 0, 1):
        pl.when(has_down)(lambda o=o: got(o, 0))
        pl.when(has_up)(lambda o=o: got(o, 3))
    lax.fori_loop(0, 4 * cores, functools.partial(norm2, (0, 3)), 0)
    clear_edges(act2)

    bias2 = column(params[core, 5], local)

    def conv2(o, carry):
        for r, h in enumerate(conv(act2, w2t, o)):
            mix[o * 2 + r] = lat[2, 1 + r, core, o].astype(F32) + (h + bias2)
        return carry

    lax.fori_loop(0, 2, conv2, 0)

    spread = select[...]
    for f in range(2):
        for r in range(2):
            for p in range(2):
                pair = [mix[f * 2 + r, pl.ds(2 * p + q, local // 4, stride=4), :].astype(BF16) for q in range(2)]
                out[f, 2 * r + p] = jnp.dot(
                    jnp.concatenate(pair, axis=1), spread, preferred_element_type=F32
                ).astype(BF16)

    for condition, copy in started:
        @pl.when(condition)
        def _(copy=copy):
            copy.wait_send()

    for o in range(4):
        pl.when(has_up)(lambda o=o: z_copy(o, True).wait_send())
        pl.when(has_down)(lambda o=o: z_copy(o, False).wait_send())
        for row in range(4):
            pl.when(row_here(row))(lambda o=o, row=row: d_copy(o, row).wait_send())


def shards(tiles, blocks, latent, n1g, n1b, w1, c1b, n2g, n2b, w2, c2b):
    frames, rows, local, wide = latent.shape
    count = tiles * blocks * 2
    groups = local // SIZE
    vmem = pl.BlockSpec(memory_space=pltpu.VMEM)
    hbm = pl.BlockSpec(memory_space=pl.ANY)
    dma = pltpu.SemaphoreType.DMA
    here = lambda v: pltpu.with_memory_space_constraint(v, pltpu.HBM)
    row = lambda v: here(v.reshape(1, local))
    return pl.pallas_call(
        functools.partial(kernel, tiles, blocks),
        out_shape=jax.ShapeDtypeStruct((frames, 2 * rows, local // 4, 2 * wide), BF16),
        in_specs=[hbm] * 9,
        out_specs=vmem,
        scratch_shapes=[
            pltpu.VMEM(w1.shape, BF16),
            pltpu.VMEM(w2.shape, BF16),
            pltpu.VMEM((3, 3 * local, 3 * C), BF16),
            pltpu.VMEM((3, 3 * local, 3 * C), BF16),
            pltpu.VMEM((3, 4, 2, 2, local, wide), BF16),
            pltpu.VMEM((6 * C, 4 * wide), BF16),
            pltpu.VMEM((4, 2, 4, local, wide), BF16),
            pltpu.VMEM((4 * C, 4 * wide), BF16),
            pltpu.VMEM((4, local, wide), F32),
            pltpu.VMEM((2 * wide, 2 * wide), BF16),
            pltpu.VMEM((2, 6, 1, local), F32),
            pltpu.VMEM((2, 1, 128), F32),
            pltpu.VMEM((2, count, 1, 128), F32),
            pltpu.VMEM((12, groups, 128), F32),
            pltpu.VMEM((12, groups, 128), F32),
            dma((8,)),
            dma((2,)),
            dma((2,)),
            dma((2, 2, 2)),
            dma((3, 2, 2)),
            dma((3, 4, 2)),
            dma((3, 4, 2)),
            dma((3, 4, 2)),
            dma((2, 4)),
            dma((4, 4)),
            dma((2, 4)),
            dma((4, 4)),
            dma((2, count)),
            dma((2, count)),
        ],
        compiler_params=pltpu.CompilerParams(
            collective_id=0, has_side_effects=True, vmem_limit_bytes=48 * 1024 * 1024
        ),
        name="block",
    )(here(latent), row(n1g), row(n1b), here(w1), row(c1b), row(n2g), row(n2b), here(w2), row(c2b))


def solution(mesh):
    return jax.shard_map(
        functools.partial(shards, mesh.shape["tile"], mesh.shape["tm"]),
        mesh=mesh,
        in_specs=(
            P(("clip", "tm"), "tile", "chan", None),
            P("chan"),
            P("chan"),
            P(None, None, None, None, "chan"),
            P("chan"),
            P("chan"),
            P("chan"),
            P(None, None, None, None, "chan"),
            P("chan"),
        ),
        out_specs=P(("clip", "tm"), "tile", "chan", None),
        check_vma=False,
    )
```

```python
import functools

import jax
import jax.numpy as jnp
from jax import lax
from jax.experimental import pallas as pl
from jax.experimental.pallas import tpu as pltpu
from jax.sharding import PartitionSpec as P

MESH = pl.DeviceIdType.MESH
C = 256
GROUPS = 32
SIZE = C // GROUPS
F32 = jnp.float32
BF16 = jnp.bfloat16


def iota(shape, dim):
    return lax.broadcasted_iota(jnp.int32, shape, dim)


def column(row, n):
    wide = jnp.broadcast_to(row, (n, row.shape[-1]))
    return jnp.sum(jnp.where(iota(wide.shape, 0) == iota(wide.shape, 1), wide, 0.0), axis=1, keepdims=True)


def kernel(
    tiles,
    blocks,
    latent,
    n1g,
    n1b,
    w1,
    c1b,
    n2g,
    n2b,
    w2,
    c2b,
    out,
    w1v,
    w2v,
    w1t,
    w2t,
    lat,
    act1,
    hid,
    act2,
    mix,
    mid,
    select,
    params,
    own_stats,
    stats,
    means,
    scales,
    l_sem,
    w_sem,
    p_sem,
    x_send,
    z_send,
    d_send,
    a_recv,
    d_recv,
    hz_send,
    hd_send,
    h_recv,
    hd_recv,
    s_send,
    s_recv,
):
    cores = 2
    count_all = tiles * blocks * cores
    tm = lax.axis_index("tm")
    tile = lax.axis_index("tile")
    core = lax.axis_index("chan")
    other = 1 - core
    me = (tm * cores + core) * tiles + tile
    local = latent.shape[2]
    wide = latent.shape[3]
    groups = local // SIZE
    rows = latent.shape[1]

    def where_is(index):
        return {"tm": index // (cores * tiles), "chan": (index // tiles) % cores, "tile": index % tiles}

    def remote(src, dst, send, recv, **device):
        return pltpu.make_async_remote_copy(
            src_ref=src, dst_ref=dst, send_sem=send, recv_sem=recv, device_id=device, device_id_type=MESH
        )

    loads = [pltpu.make_async_copy(latent.at[:, r], lat.at[2, 1 + r, core], l_sem.at[r]) for r in (0, 1)]
    loads += [
        pltpu.make_async_copy(ref, params.at[core, i], l_sem.at[2 + i])
        for i, ref in enumerate((n1g, n1b, n2g, n2b, c1b, c2b))
    ]
    load1 = pltpu.make_async_copy(w1, w1v, w_sem.at[0])
    load2 = pltpu.make_async_copy(w2, w2v, w_sem.at[1])
    barrier = pltpu.get_barrier_semaphore()

    def greet(step, carry):
        pl.semaphore_signal(
            barrier, inc=1, device_id=where_is(lax.rem(me + step, count_all)), device_id_type=MESH
        )
        return carry

    lax.fori_loop(1, count_all, greet, 0)
    for copy in loads:
        copy.start()
    load1.start()
    load2.start()
    for copy in loads:
        copy.wait()

    started = []

    def go(condition, copy):
        @pl.when(condition)
        def _():
            copy.start()

        started.append((condition, copy))

    always = core >= 0
    has_up = tile < tiles - 1
    has_down = tile > 0
    slots = [s for s in range(3) if blocks > 2 - s]
    before = [s for s in slots if s < 2]

    def lat_copy(s, row, f, to_s, to_row, send, recv, **device):
        return remote(lat.at[s, row, core, f], lat.at[to_s, to_row, core, f], send, recv, **device)

    lanes = iota((groups, 128), 1)
    subs = iota((groups, 128), 0)

    def make_stats(which, field):
        row = jnp.zeros((1, 128), F32)
        for f in (0, 1):
            total = jnp.zeros((groups, wide), F32)
            square = jnp.zeros((groups, wide), F32)
            for r in (0, 1):
                v = field(f, r).reshape(groups, SIZE, wide)
                total = total + jnp.sum(v, axis=1)
                square = square + jnp.sum(v * v, axis=1)
            for kind, part in enumerate((total, square)):
                col = jnp.sum(part, axis=1, keepdims=True)
                at = kind * 2 * groups + f * groups
                row = row + jnp.sum(jnp.where(lanes == subs + at, col, 0.0), axis=0, keepdims=True)
        own_stats[which] = row
        stats[which, me] = row

    def send_stats(which):
        def send(step, carry):
            to = lax.rem(me + step, count_all)
            remote(own_stats.at[which], stats.at[which, me], s_send.at[which, to], s_recv.at[which, me],
                   **where_is(to)).start()
            return carry

        lax.fori_loop(1, count_all, send, 0)

    def wait_stats(which):
        def wait(step, carry):
            to = lax.rem(me + step, count_all)
            remote(own_stats.at[which], stats.at[which, to], s_send.at[which, to], s_recv.at[which, to],
                   **where_is(to)).wait()
            return carry

        lax.fori_loop(1, count_all, wait, 0)

    def make_norms(which, frames):
        ahead = frames // 2 - 1
        per_block = []
        for b in range(blocks):
            for c in range(cores):
                first = jnp.sum(stats[which, pl.ds((b * cores + c) * tiles, tiles)], axis=0)
                both = first + pltpu.roll(first, 128 - groups, 1)
                per_block.append((b, c, first, both))
        for e in range(frames):
            block = tm - ahead + e // 2
            later = jnp.logical_and(block >= 0, e % 2 == 1)
            block = jnp.maximum(block, 0)
            number = (block * 2 + later.astype(jnp.int32) + 1).astype(F32)
            count = number * float(rows * tiles * SIZE * wide)
            for c in range(cores):
                run = jnp.zeros((1, 128), F32)
                for b, cc, first, both in per_block:
                    if cc == c:
                        whole = jnp.logical_or(b < block, jnp.logical_and(b == block, later))
                        run = run + jnp.where(whole, both, jnp.where(b == block, first, 0.0))
                mean = run / count
                var = pltpu.roll(mean, 128 - 2 * groups, 1) - mean * mean
                scale = 1.0 / jnp.sqrt(var + 1e-06)
                diagonal = lanes == subs
                for ref, value in ((means, mean), (scales, scale)):
                    col = jnp.sum(jnp.where(diagonal, jnp.broadcast_to(value, lanes.shape), 0.0), axis=1,
                                  keepdims=True)
                    ref[e * cores + c] = jnp.broadcast_to(col, (groups, 128))

    def per_channel(ref, at):
        v = ref[at]
        return jnp.broadcast_to(v[:, None, :], (groups, SIZE, 128)).reshape(local, 128)

    def flip(src, dst):
        def one(j, carry):
            for i in range(3):
                for k in range(3):
                    dst[j, k * local:(k + 1) * local, i * C:(i + 1) * C] = src[i, j, k].T
            return carry

        lax.fori_loop(0, 3, one, 0)

    def silu_of_twice(half):
        return half + half * jnp.tanh(half)

    def clear_edges(act):
        for side, row in ((has_down, 0), (has_up, 3)):
            @pl.when(jnp.logical_not(side))
            def _(row=row):
                act[:, row * wide:(row + 1) * wide] = jnp.zeros((act.shape[0], wide), BF16)

    def tap(act, wt, o, j):
        return jnp.dot(
            wt[j], act[pl.ds(pl.multiple_of(o * C, C), 3 * C), j * wide:(j + 2) * wide],
            preferred_element_type=F32,
        )

    def middle(act, wt, first, last):
        def one(o, carry):
            mid[o] = tap(act, wt, o, 1)
            return carry

        lax.fori_loop(first, last, one, 0)

    def conv(act, wt, o):
        acc = mid[o] + tap(act, wt, o, 0) + tap(act, wt, o, 2)
        lane = iota((local, wide), 1)
        result = []
        for r in range(2):
            a = [acc[k * local:(k + 1) * local, r * wide:(r + 1) * wide] for k in range(3)]
            left = jnp.where(lane == 0, 0.0, pltpu.roll(a[0], 1, 1))
            right = jnp.where(lane == wide - 1, 0.0, pltpu.roll(a[2], wide - 1, 1))
            result.append(a[1] + left + right)
        return result

    make_stats(0, lambda f, r: lat[2, 1 + r, core, f].astype(F32))
    pl.semaphore_wait(barrier, count_all - 1)
    send_stats(0)

    for s in reversed(before):
        for f in (0, 1):
            for r in (0, 1):
                go(tm + (2 - s) < blocks,
                   lat_copy(2, 1 + r, f, s, 1 + r, x_send.at[s, r, f], a_recv.at[s, 1 + r, f], tm=tm + (2 - s)))
    for f in (0, 1):
        go(has_up, lat_copy(2, 2, f, 2, 0, z_send.at[2, 0, f], a_recv.at[2, 0, f], tile=tile + 1))
        go(has_down, lat_copy(2, 1, f, 2, 3, z_send.at[2, 1, f], a_recv.at[2, 3, f], tile=tile - 1))
    for f in (0, 1):
        for r in (1, 2):
            go(always, lat_copy(2, r, f, 2, r, d_send.at[2, r, f], d_recv.at[2, r, f], chan=other))
    go(always, remote(params.at[core], params.at[core], p_sem.at[0], p_sem.at[1], chan=other))

    a, b = iota((2 * wide, 2 * wide), 0), iota((2 * wide, 2 * wide), 1)
    select[...] = jnp.where(b == 2 * (a % wide) + a // wide, 1.0, 0.0).astype(BF16)
    load1.wait()
    flip(w1v, w1t)
    load2.wait()
    flip(w2v, w2t)

    def arrived(s, row, f, condition):
        copy = lat_copy(s, row, f, s, row, d_send.at[s, row, f], d_recv.at[s, row, f], chan=other)

        @pl.when(condition)
        def _():
            lat_copy(s, row, f, s, row, d_send.at[s, row, f], a_recv.at[s, row, f], chan=other).wait_recv()
            copy.start()

        started.append((condition, copy))

    def from_other(s, row, f, condition):
        @pl.when(condition)
        def _():
            remote(lat.at[s, row, core, f], lat.at[s, row, other, f], d_send.at[s, row, f], d_recv.at[s, row, f],
                   chan=other).wait_recv()

    def row_here(row):
        return has_down if row == 0 else has_up if row == 3 else always

    for s in reversed(before):
        here = tm >= 2 - s
        for f in (0, 1):
            for r in (0, 1):
                arrived(s, 1 + r, f, here)
                side, row, to = ((has_down, 3, tile - 1), (has_up, 0, tile + 1))[r]
                go(jnp.logical_and(here, side),
                   lat_copy(s, 1 + r, f, s, row, z_send.at[s, 1 - r, f], a_recv.at[s, row, f], tile=to))

    for f in (0, 1):
        for row in (0, 3):
            arrived(2, row, f, row_here(row))

    wait_stats(0)
    make_norms(0, 6)
    remote(params.at[core], params.at[other], p_sem.at[0], p_sem.at[1], chan=other).wait_recv()
    for f in (0, 1):
        for row in range(4):
            from_other(2, row, f, row_here(row))

    def norm1(first, rows_of):
        def one(step, carry):
            e, c = step // cores, step % cores
            s, f = e // 2, e % 2
            f = jnp.where(tm - 2 + s < 0, 0, f)
            s = jnp.maximum(s, 2 - tm)
            gain = per_channel(scales, step) * column(0.5 * params[c, 0], local)
            bias = column(0.5 * params[c, 1], local) - per_channel(means, step) * gain
            for row in rows_of:
                v = silu_of_twice(lat[s, row, c, f].astype(F32) * gain + bias)
                act1[pl.ds(pl.multiple_of(step * local, local), local), row * wide:(row + 1) * wide] = v.astype(BF16)
            return carry

        lax.fori_loop(first * cores, (first + 2) * cores, one, 0)

    def norm1_first(rows_of):
        def repeat():
            for row in rows_of:
                at = slice(row * wide, (row + 1) * wide)
                first = act1[2 * C:3 * C, at]
                act1[0:C, at] = first
                act1[C:2 * C, at] = first

        if blocks > 2:
            @pl.when(tm >= 2)
            def _():
                norm1(0, rows_of)

            pl.when(tm < 2)(repeat)
        else:
            repeat()

    norm1(4, range(4))
    for s in before:
        for f in (0, 1):
            for row in (1, 2):
                from_other(s, row, f, tm >= 2 - s)
    norm1(2, (1, 2))
    norm1_first((1, 2))
    middle(act1, w1t, 2, 4)
    for s in before:
        for f in (0, 1):
            for row in (0, 3):
                arrived(s, row, f, jnp.logical_and(tm >= 2 - s, row_here(row)))
    middle(act1, w1t, 0, 2)
    for s in before:
        for f in (0, 1):
            for row in (0, 3):
                from_other(s, row, f, jnp.logical_and(tm >= 2 - s, row_here(row)))
    norm1(2, (0, 3))
    norm1_first((0, 3))
    clear_edges(act1)

    def z_copy(o, up):
        at, row, to, landed = (0, 2, tile + 1, 0) if up else (1, 1, tile - 1, 3)
        return remote(hid.at[row, core, o], hid.at[landed, core, o], hz_send.at[at, o], h_recv.at[at, o], tile=to)

    def d_copy(o, row):
        return remote(hid.at[row, core, o], hid.at[row, core, o], hd_send.at[row, o], hd_recv.at[row, o], chan=other)

    def conv1(o, carry):
        for r, h in enumerate(conv(act1, w1t, o)):
            hid[1 + r, core, o] = h.astype(BF16)

            @pl.when(o >= 2)
            def _():
                mix[jnp.maximum(o - 2, 0) * 2 + r] = h

        pl.when(has_up)(lambda: z_copy(o, True).start())
        pl.when(has_down)(lambda: z_copy(o, False).start())
        d_copy(o, 1).start()
        d_copy(o, 2).start()
        return carry

    lax.fori_loop(2, 4, conv1, 0)
    bias1 = column(params[core, 4], local)
    make_stats(1, lambda f, r: mix[f * 2 + r] + bias1)
    send_stats(1)
    lax.fori_loop(0, 2, conv1, 0)

    for o in (2, 3, 0, 1):
        for at, row in ((0, 0), (1, 3)):
            @pl.when(row_here(row))
            def _(at=at, row=row, o=o):
                remote(hid.at[row, core, o], hid.at[row, core, o], hd_send.at[row, o], h_recv.at[at, o],
                       chan=other).wait_recv()
                d_copy(o, row).start()
    wait_stats(1)
    make_norms(1, 4)

    def got(o, row):
        remote(hid.at[row, core, o], hid.at[row, other, o], hd_send.at[row, o], hd_recv.at[row, o],
               chan=other).wait_recv()

    def norm2(rows_of, step, carry):
        e, c = step // cores, step % cores
        gain = per_channel(scales, step) * column(0.5 * params[c, 2], local)
        bias = column(0.5 * params[c, 3], local) + (column(params[c, 4], local) - per_channel(means, step)) * gain
        for row in rows_of:
            v = silu_of_twice(hid[row, c, e].astype(F32) * gain + bias)
            act2[pl.ds(pl.multiple_of(step * local, local), local), row * wide:(row + 1) * wide] = v.astype(BF16)
        return carry

    for o in (2, 3, 0, 1):
        got(o, 1)
        got(o, 2)
    lax.fori_loop(0, 4 * cores, functools.partial(norm2, (1, 2)), 0)
    middle(act2, w2t, 0, 2)
    for o in (2, 3, 0, 1):
        pl.when(has_down)(lambda o=o: got(o, 0))
        pl.when(has_up)(lambda o=o: got(o, 3))
    lax.fori_loop(0, 4 * cores, functools.partial(norm2, (0, 3)), 0)
    clear_edges(act2)

    bias2 = column(params[core, 5], local)

    def conv2(o, carry):
        for r, h in enumerate(conv(act2, w2t, o)):
            mix[o * 2 + r] = lat[2, 1 + r, core, o].astype(F32) + (h + bias2)
        return carry

    lax.fori_loop(0, 2, conv2, 0)

    spread = select[...]
    for f in range(2):
        for r in range(2):
            for p in range(2):
                pair = [mix[f * 2 + r, pl.ds(2 * p + q, local // 4, stride=4), :].astype(BF16) for q in range(2)]
                out[f, 2 * r + p] = jnp.dot(
                    jnp.concatenate(pair, axis=1), spread, preferred_element_type=F32
                ).astype(BF16)

    for condition, copy in started:
        @pl.when(condition)
        def _(copy=copy):
            copy.wait_send()

    for o in range(4):
        pl.when(has_up)(lambda o=o: z_copy(o, True).wait_send())
        pl.when(has_down)(lambda o=o: z_copy(o, False).wait_send())
        for row in range(4):
            pl.when(row_here(row))(lambda o=o, row=row: d_copy(o, row).wait_send())


def shards(tiles, blocks, latent, n1g, n1b, w1, c1b, n2g, n2b, w2, c2b):
    frames, rows, local, wide = latent.shape
    count = tiles * blocks * 2
    groups = local // SIZE
    vmem = pl.BlockSpec(memory_space=pltpu.VMEM)
    hbm = pl.BlockSpec(memory_space=pl.ANY)
    dma = pltpu.SemaphoreType.DMA
    here = lambda v: pltpu.with_memory_space_constraint(v, pltpu.HBM)
    row = lambda v: here(v.reshape(1, local))
    return pl.pallas_call(
        functools.partial(kernel, tiles, blocks),
        out_shape=jax.ShapeDtypeStruct((frames, 2 * rows, local // 4, 2 * wide), BF16),
        in_specs=[hbm] * 9,
        out_specs=vmem,
        scratch_shapes=[
            pltpu.VMEM(w1.shape, BF16),
            pltpu.VMEM(w2.shape, BF16),
            pltpu.VMEM((3, 3 * local, 3 * C), BF16),
            pltpu.VMEM((3, 3 * local, 3 * C), BF16),
            pltpu.VMEM((3, 4, 2, 2, local, wide), BF16),
            pltpu.VMEM((6 * C, 4 * wide), BF16),
            pltpu.VMEM((4, 2, 4, local, wide), BF16),
            pltpu.VMEM((4 * C, 4 * wide), BF16),
            pltpu.VMEM((4, local, wide), F32),
            pltpu.VMEM((4, 3 * local, 2 * wide), F32),
            pltpu.VMEM((2 * wide, 2 * wide), BF16),
            pltpu.VMEM((2, 6, 1, local), F32),
            pltpu.VMEM((2, 1, 128), F32),
            pltpu.VMEM((2, count, 1, 128), F32),
            pltpu.VMEM((12, groups, 128), F32),
            pltpu.VMEM((12, groups, 128), F32),
            dma((8,)),
            dma((2,)),
            dma((2,)),
            dma((2, 2, 2)),
            dma((3, 2, 2)),
            dma((3, 4, 2)),
            dma((3, 4, 2)),
            dma((3, 4, 2)),
            dma((2, 4)),
            dma((4, 4)),
            dma((2, 4)),
            dma((4, 4)),
            dma((2, count)),
            dma((2, count)),
        ],
        compiler_params=pltpu.CompilerParams(
            collective_id=0, has_side_effects=True, vmem_limit_bytes=48 * 1024 * 1024
        ),
        name="block",
    )(here(latent), row(n1g), row(n1b), here(w1), row(c1b), row(n2g), row(n2b), here(w2), row(c2b))


def solution(mesh):
    return jax.shard_map(
        functools.partial(shards, mesh.shape["tile"], mesh.shape["tm"]),
        mesh=mesh,
        in_specs=(
            P(("clip", "tm"), "tile", "chan", None),
            P("chan"),
            P("chan"),
            P(None, None, None, None, "chan"),
            P("chan"),
            P("chan"),
            P("chan"),
            P(None, None, None, None, "chan"),
            P("chan"),
        ),
        out_specs=P(("clip", "tm"), "tile", "chan", None),
        check_vma=False,
    )
```

```python
import functools

import jax
import jax.numpy as jnp
from jax import lax
from jax.experimental import pallas as pl
from jax.experimental.pallas import tpu as pltpu
from jax.sharding import PartitionSpec as P

MESH = pl.DeviceIdType.MESH
C = 256
GROUPS = 32
SIZE = C // GROUPS
F32 = jnp.float32
BF16 = jnp.bfloat16


def iota(shape, dim):
    return lax.broadcasted_iota(jnp.int32, shape, dim)


def column(row, n):
    wide = jnp.broadcast_to(row, (n, row.shape[-1]))
    return jnp.sum(jnp.where(iota(wide.shape, 0) == iota(wide.shape, 1), wide, 0.0), axis=1, keepdims=True)


def kernel(
    tiles,
    blocks,
    latent,
    n1g,
    n1b,
    w1,
    c1b,
    n2g,
    n2b,
    w2,
    c2b,
    out,
    w1v,
    w2v,
    w1t,
    w2t,
    lat,
    act1,
    hid,
    act2,
    mix,
    mid,
    select,
    params,
    own_stats,
    stats,
    means,
    scales,
    l_sem,
    w_sem,
    p_sem,
    x_send,
    z_send,
    d_send,
    a_recv,
    d_recv,
    hz_send,
    hd_send,
    h_recv,
    hd_recv,
    s_send,
    s_recv,
):
    cores = 2
    count_all = tiles * blocks * cores
    few = count_all <= 16
    tm = lax.axis_index("tm")
    tile = lax.axis_index("tile")
    core = lax.axis_index("chan")
    other = 1 - core
    me = (tm * cores + core) * tiles + tile
    local = latent.shape[2]
    wide = latent.shape[3]
    groups = local // SIZE
    rows = latent.shape[1]

    def where_is(index):
        return {"tm": index // (cores * tiles), "chan": (index // tiles) % cores, "tile": index % tiles}

    def remote(src, dst, send, recv, **device):
        return pltpu.make_async_remote_copy(
            src_ref=src, dst_ref=dst, send_sem=send, recv_sem=recv, device_id=device, device_id_type=MESH
        )

    loads = [pltpu.make_async_copy(latent.at[:, r], lat.at[2, 1 + r, core], l_sem.at[r]) for r in (0, 1)]
    loads += [
        pltpu.make_async_copy(ref, params.at[core, i], l_sem.at[2 + i])
        for i, ref in enumerate((n1g, n1b, n2g, n2b, c1b, c2b))
    ]
    load1 = pltpu.make_async_copy(w1, w1v, w_sem.at[0])
    load2 = pltpu.make_async_copy(w2, w2v, w_sem.at[1])
    barrier = pltpu.get_barrier_semaphore()

    def greet(step, carry):
        pl.semaphore_signal(
            barrier, inc=1, device_id=where_is(lax.rem(me + step, count_all)), device_id_type=MESH
        )
        return carry

    lax.fori_loop(1, count_all, greet, 0, unroll=few)
    for copy in loads:
        copy.start()
    load1.start()
    load2.start()
    for copy in loads:
        copy.wait()

    started = []

    def go(condition, copy):
        @pl.when(condition)
        def _():
            copy.start()

        started.append((condition, copy))

    always = core >= 0
    has_up = tile < tiles - 1
    has_down = tile > 0
    slots = [s for s in range(3) if blocks > 2 - s]
    before = [s for s in slots if s < 2]

    def lat_copy(s, row, f, to_s, to_row, send, recv, **device):
        return remote(lat.at[s, row, core, f], lat.at[to_s, to_row, core, f], send, recv, **device)

    lanes = iota((groups, 128), 1)
    subs = iota((groups, 128), 0)

    def make_stats(which, field):
        row = jnp.zeros((1, 128), F32)
        for f in (0, 1):
            total = jnp.zeros((groups, wide), F32)
            square = jnp.zeros((groups, wide), F32)
            for r in (0, 1):
                v = field(f, r).reshape(groups, SIZE, wide)
                total = total + jnp.sum(v, axis=1)
                square = square + jnp.sum(v * v, axis=1)
            for kind, part in enumerate((total, square)):
                col = jnp.sum(part, axis=1, keepdims=True)
                at = kind * 2 * groups + f * groups
                row = row + jnp.sum(jnp.where(lanes == subs + at, col, 0.0), axis=0, keepdims=True)
        own_stats[which] = row
        stats[which, me] = row

    def send_stats(which):
        def send(step, carry):
            to = lax.rem(me + step, count_all)
            remote(own_stats.at[which], stats.at[which, me], s_send.at[which, to], s_recv.at[which, me],
                   **where_is(to)).start()
            return carry

        lax.fori_loop(1, count_all, send, 0, unroll=few)

    def wait_stats(which):
        def wait(step, carry):
            to = lax.rem(me + step, count_all)
            remote(own_stats.at[which], stats.at[which, to], s_send.at[which, to], s_recv.at[which, to],
                   **where_is(to)).wait()
            return carry

        lax.fori_loop(1, count_all, wait, 0, unroll=few)

    def make_norms(which, frames):
        ahead = frames // 2 - 1
        per_block = []
        for b in range(blocks):
            for c in range(cores):
                first = jnp.sum(stats[which, pl.ds((b * cores + c) * tiles, tiles)], axis=0)
                both = first + pltpu.roll(first, 128 - groups, 1)
                per_block.append((b, c, first, both))
        for e in range(frames):
            block = tm - ahead + e // 2
            later = jnp.logical_and(block >= 0, e % 2 == 1)
            block = jnp.maximum(block, 0)
            number = (block * 2 + later.astype(jnp.int32) + 1).astype(F32)
            count = number * float(rows * tiles * SIZE * wide)
            for c in range(cores):
                run = jnp.zeros((1, 128), F32)
                for b, cc, first, both in per_block:
                    if cc == c:
                        whole = jnp.logical_or(b < block, jnp.logical_and(b == block, later))
                        run = run + jnp.where(whole, both, jnp.where(b == block, first, 0.0))
                mean = run / count
                var = pltpu.roll(mean, 128 - 2 * groups, 1) - mean * mean
                scale = 1.0 / jnp.sqrt(var + 1e-06)
                diagonal = lanes == subs
                for ref, value in ((means, mean), (scales, scale)):
                    col = jnp.sum(jnp.where(diagonal, jnp.broadcast_to(value, lanes.shape), 0.0), axis=1,
                                  keepdims=True)
                    ref[e * cores + c] = jnp.broadcast_to(col, (groups, 128))

    def per_channel(ref, at):
        v = ref[at]
        return jnp.broadcast_to(v[:, None, :], (groups, SIZE, 128)).reshape(local, 128)

    def flip(src, dst):
        def one(j, carry):
            for i in range(3):
                for k in range(3):
                    dst[j, k * local:(k + 1) * local, i * C:(i + 1) * C] = src[i, j, k].T
            return carry

        lax.fori_loop(0, 3, one, 0)

    def silu_of_twice(half):
        return half + half * jnp.tanh(half)

    def clear_edges(act):
        for side, row in ((has_down, 0), (has_up, 3)):
            @pl.when(jnp.logical_not(side))
            def _(row=row):
                act[:, row * wide:(row + 1) * wide] = jnp.zeros((act.shape[0], wide), BF16)

    def tap(act, wt, o, j):
        return jnp.dot(
            wt[j], act[pl.ds(pl.multiple_of(o * C, C), 3 * C), j * wide:(j + 2) * wide],
            preferred_element_type=F32,
        )

    def middle(act, wt, first, last):
        def one(o, carry):
            mid[o] = tap(act, wt, o, 1)
            return carry

        lax.fori_loop(first, last, one, 0)

    def conv(act, wt, o):
        acc = mid[o] + tap(act, wt, o, 0) + tap(act, wt, o, 2)
        lane = iota((local, wide), 1)
        result = []
        for r in range(2):
            a = [acc[k * local:(k + 1) * local, r * wide:(r + 1) * wide] for k in range(3)]
            left = jnp.where(lane == 0, 0.0, pltpu.roll(a[0], 1, 1))
            right = jnp.where(lane == wide - 1, 0.0, pltpu.roll(a[2], wide - 1, 1))
            result.append(a[1] + left + right)
        return result

    make_stats(0, lambda f, r: lat[2, 1 + r, core, f].astype(F32))
    pl.semaphore_wait(barrier, count_all - 1)
    send_stats(0)

    for s in reversed(before):
        for f in (0, 1):
            for r in (0, 1):
                go(tm + (2 - s) < blocks,
                   lat_copy(2, 1 + r, f, s, 1 + r, x_send.at[s, r, f], a_recv.at[s, 1 + r, f], tm=tm + (2 - s)))
    for f in (0, 1):
        go(has_up, lat_copy(2, 2, f, 2, 0, z_send.at[2, 0, f], a_recv.at[2, 0, f], tile=tile + 1))
        go(has_down, lat_copy(2, 1, f, 2, 3, z_send.at[2, 1, f], a_recv.at[2, 3, f], tile=tile - 1))
    for f in (0, 1):
        for r in (1, 2):
            go(always, lat_copy(2, r, f, 2, r, d_send.at[2, r, f], d_recv.at[2, r, f], chan=other))
    go(always, remote(params.at[core], params.at[core], p_sem.at[0], p_sem.at[1], chan=other))

    a, b = iota((2 * wide, 2 * wide), 0), iota((2 * wide, 2 * wide), 1)
    select[...] = jnp.where(b == 2 * (a % wide) + a // wide, 1.0, 0.0).astype(BF16)
    load1.wait()
    flip(w1v, w1t)
    load2.wait()
    flip(w2v, w2t)

    def arrived(s, row, f, condition):
        copy = lat_copy(s, row, f, s, row, d_send.at[s, row, f], d_recv.at[s, row, f], chan=other)

        @pl.when(condition)
        def _():
            lat_copy(s, row, f, s, row, d_send.at[s, row, f], a_recv.at[s, row, f], chan=other).wait_recv()
            copy.start()

        started.append((condition, copy))

    def from_other(s, row, f, condition):
        @pl.when(condition)
        def _():
            remote(lat.at[s, row, core, f], lat.at[s, row, other, f], d_send.at[s, row, f], d_recv.at[s, row, f],
                   chan=other).wait_recv()

    def row_here(row):
        return has_down if row == 0 else has_up if row == 3 else always

    for s in reversed(before):
        here = tm >= 2 - s
        for f in (0, 1):
            for r in (0, 1):
                arrived(s, 1 + r, f, here)
                side, row, to = ((has_down, 3, tile - 1), (has_up, 0, tile + 1))[r]
                go(jnp.logical_and(here, side),
                   lat_copy(s, 1 + r, f, s, row, z_send.at[s, 1 - r, f], a_recv.at[s, row, f], tile=to))

    for f in (0, 1):
        for row in (0, 3):
            arrived(2, row, f, row_here(row))

    wait_stats(0)
    make_norms(0, 6)
    remote(params.at[core], params.at[other], p_sem.at[0], p_sem.at[1], chan=other).wait_recv()
    for f in (0, 1):
        for row in range(4):
            from_other(2, row, f, row_here(row))

    def norm1(first, rows_of):
        def one(step, carry):
            e, c = step // cores, step % cores
            s, f = e // 2, e % 2
            f = jnp.where(tm - 2 + s < 0, 0, f)
            s = jnp.maximum(s, 2 - tm)
            gain = per_channel(scales, step) * column(0.5 * params[c, 0], local)
            bias = column(0.5 * params[c, 1], local) - per_channel(means, step) * gain
            for row in rows_of:
                v = silu_of_twice(lat[s, row, c, f].astype(F32) * gain + bias)
                act1[pl.ds(pl.multiple_of(step * local, local), local), row * wide:(row + 1) * wide] = v.astype(BF16)
            return carry

        lax.fori_loop(first * cores, (first + 2) * cores, one, 0)

    def norm1_first(rows_of):
        def repeat():
            for row in rows_of:
                at = slice(row * wide, (row + 1) * wide)
                first = act1[2 * C:3 * C, at]
                act1[0:C, at] = first
                act1[C:2 * C, at] = first

        if blocks > 2:
            @pl.when(tm >= 2)
            def _():
                norm1(0, rows_of)

            pl.when(tm < 2)(repeat)
        else:
            repeat()

    norm1(4, range(4))
    for s in before:
        for f in (0, 1):
            for row in (1, 2):
                from_other(s, row, f, tm >= 2 - s)
    norm1(2, (1, 2))
    norm1_first((1, 2))
    middle(act1, w1t, 2, 4)
    for s in before:
        for f in (0, 1):
            for row in (0, 3):
                arrived(s, row, f, jnp.logical_and(tm >= 2 - s, row_here(row)))
    middle(act1, w1t, 0, 2)
    for s in before:
        for f in (0, 1):
            for row in (0, 3):
                from_other(s, row, f, jnp.logical_and(tm >= 2 - s, row_here(row)))
    norm1(2, (0, 3))
    norm1_first((0, 3))
    clear_edges(act1)

    def z_copy(o, up):
        at, row, to, landed = (0, 2, tile + 1, 0) if up else (1, 1, tile - 1, 3)
        return remote(hid.at[row, core, o], hid.at[landed, core, o], hz_send.at[at, o], h_recv.at[at, o], tile=to)

    def d_copy(o, row):
        return remote(hid.at[row, core, o], hid.at[row, core, o], hd_send.at[row, o], hd_recv.at[row, o], chan=other)

    def conv1(o, carry):
        for r, h in enumerate(conv(act1, w1t, o)):
            hid[1 + r, core, o] = h.astype(BF16)

            @pl.when(o >= 2)
            def _():
                mix[jnp.maximum(o - 2, 0) * 2 + r] = h

        pl.when(has_up)(lambda: z_copy(o, True).start())
        pl.when(has_down)(lambda: z_copy(o, False).start())
        d_copy(o, 1).start()
        d_copy(o, 2).start()
        return carry

    lax.fori_loop(2, 4, conv1, 0)
    bias1 = column(params[core, 4], local)
    make_stats(1, lambda f, r: mix[f * 2 + r] + bias1)
    send_stats(1)
    lax.fori_loop(0, 2, conv1, 0)

    for o in (2, 3, 0, 1):
        for at, row in ((0, 0), (1, 3)):
            @pl.when(row_here(row))
            def _(at=at, row=row, o=o):
                remote(hid.at[row, core, o], hid.at[row, core, o], hd_send.at[row, o], h_recv.at[at, o],
                       chan=other).wait_recv()
                d_copy(o, row).start()
    wait_stats(1)
    make_norms(1, 4)

    def got(o, row):
        remote(hid.at[row, core, o], hid.at[row, other, o], hd_send.at[row, o], hd_recv.at[row, o],
               chan=other).wait_recv()

    def norm2(rows_of, step, carry):
        e, c = step // cores, step % cores
        gain = per_channel(scales, step) * column(0.5 * params[c, 2], local)
        bias = column(0.5 * params[c, 3], local) + (column(params[c, 4], local) - per_channel(means, step)) * gain
        for row in rows_of:
            v = silu_of_twice(hid[row, c, e].astype(F32) * gain + bias)
            act2[pl.ds(pl.multiple_of(step * local, local), local), row * wide:(row + 1) * wide] = v.astype(BF16)
        return carry

    for o in (2, 3, 0, 1):
        got(o, 1)
        got(o, 2)
    lax.fori_loop(0, 4 * cores, functools.partial(norm2, (1, 2)), 0)
    middle(act2, w2t, 0, 2)
    for o in (2, 3, 0, 1):
        pl.when(has_down)(lambda o=o: got(o, 0))
        pl.when(has_up)(lambda o=o: got(o, 3))
    lax.fori_loop(0, 4 * cores, functools.partial(norm2, (0, 3)), 0)
    clear_edges(act2)

    bias2 = column(params[core, 5], local)

    def conv2(o, carry):
        for r, h in enumerate(conv(act2, w2t, o)):
            mix[o * 2 + r] = lat[2, 1 + r, core, o].astype(F32) + (h + bias2)
        return carry

    lax.fori_loop(0, 2, conv2, 0)

    spread = select[...]
    for f in range(2):
        for r in range(2):
            for p in range(2):
                pair = [mix[f * 2 + r, pl.ds(2 * p + q, local // 4, stride=4), :].astype(BF16) for q in range(2)]
                out[f, 2 * r + p] = jnp.dot(
                    jnp.concatenate(pair, axis=1), spread, preferred_element_type=F32
                ).astype(BF16)

    for condition, copy in started:
        @pl.when(condition)
        def _(copy=copy):
            copy.wait_send()

    for o in range(4):
        pl.when(has_up)(lambda o=o: z_copy(o, True).wait_send())
        pl.when(has_down)(lambda o=o: z_copy(o, False).wait_send())
        for row in range(4):
            pl.when(row_here(row))(lambda o=o, row=row: d_copy(o, row).wait_send())


def shards(tiles, blocks, latent, n1g, n1b, w1, c1b, n2g, n2b, w2, c2b):
    frames, rows, local, wide = latent.shape
    count = tiles * blocks * 2
    groups = local // SIZE
    vmem = pl.BlockSpec(memory_space=pltpu.VMEM)
    hbm = pl.BlockSpec(memory_space=pl.ANY)
    dma = pltpu.SemaphoreType.DMA
    here = lambda v: pltpu.with_memory_space_constraint(v, pltpu.HBM)
    row = lambda v: here(v.reshape(1, local))
    return pl.pallas_call(
        functools.partial(kernel, tiles, blocks),
        out_shape=jax.ShapeDtypeStruct((frames, 2 * rows, local // 4, 2 * wide), BF16),
        in_specs=[hbm] * 9,
        out_specs=vmem,
        scratch_shapes=[
            pltpu.VMEM(w1.shape, BF16),
            pltpu.VMEM(w2.shape, BF16),
            pltpu.VMEM((3, 3 * local, 3 * C), BF16),
            pltpu.VMEM((3, 3 * local, 3 * C), BF16),
            pltpu.VMEM((3, 4, 2, 2, local, wide), BF16),
            pltpu.VMEM((6 * C, 4 * wide), BF16),
            pltpu.VMEM((4, 2, 4, local, wide), BF16),
            pltpu.VMEM((4 * C, 4 * wide), BF16),
            pltpu.VMEM((4, local, wide), F32),
            pltpu.VMEM((4, 3 * local, 2 * wide), F32),
            pltpu.VMEM((2 * wide, 2 * wide), BF16),
            pltpu.VMEM((2, 6, 1, local), F32),
            pltpu.VMEM((2, 1, 128), F32),
            pltpu.VMEM((2, count, 1, 128), F32),
            pltpu.VMEM((12, groups, 128), F32),
            pltpu.VMEM((12, groups, 128), F32),
            dma((8,)),
            dma((2,)),
            dma((2,)),
            dma((2, 2, 2)),
            dma((3, 2, 2)),
            dma((3, 4, 2)),
            dma((3, 4, 2)),
            dma((3, 4, 2)),
            dma((2, 4)),
            dma((4, 4)),
            dma((2, 4)),
            dma((4, 4)),
            dma((2, count)),
            dma((2, count)),
        ],
        compiler_params=pltpu.CompilerParams(
            collective_id=0, has_side_effects=True, vmem_limit_bytes=48 * 1024 * 1024
        ),
        name="block",
    )(here(latent), row(n1g), row(n1b), here(w1), row(c1b), row(n2g), row(n2b), here(w2), row(c2b))


def solution(mesh):
    return jax.shard_map(
        functools.partial(shards, mesh.shape["tile"], mesh.shape["tm"]),
        mesh=mesh,
        in_specs=(
            P(("clip", "tm"), "tile", "chan", None),
            P("chan"),
            P("chan"),
            P(None, None, None, None, "chan"),
            P("chan"),
            P("chan"),
            P("chan"),
            P(None, None, None, None, "chan"),
            P("chan"),
        ),
        out_specs=P(("clip", "tm"), "tile", "chan", None),
        check_vma=False,
    )
```
